32 devices in a mesh: pipe: 2 (over core), dp: 4 (over y, x), tensor: 4 (over z).
Axes of the slice: x: 2, y: 2, z: 4, core: 2. Of those that a mesh axis runs over, the one named last changes fastest.
Arguments:
- ends: float32 [2, 8, 512, 1024], P('pipe', 'dp', 'tensor'), may hold values from -6 to 6
- mix_in: bfloat16 [2, 1024, 2, 1024], P('pipe', 'dp', None, 'tensor'), may hold values from -0.1875 to 0.1875
- mix_out: bfloat16 [2, 1024, 1024], P('pipe', 'tensor', 'dp'), may hold values from -0.75 to 0.75
- gate_up: bfloat16 [2, 1024, 2, 4608], P('pipe', 'dp', None, 'tensor'), may hold values from -0.1875 to 0.1875
- down: bfloat16 [2, 4608, 1024], P('pipe', 'tensor', 'dp'), may hold values from -0.09375 to 0.09375
- value_weight: bfloat16 [1024, 1024], P(('pipe', 'dp'), 'tensor'), may hold values from -0.1875 to 0.1875
- gains_one: float32 [2, 1024], replicated, may hold values from 0.25 to 1.75
- gains_two: float32 [2, 1024], replicated, may hold values from 0.25 to 1.75
- conv_kernel: float32 [3, 1024], replicated, may hold values from -1 to 1
- qk_gains: float32 [2, 64], replicated, may hold values from 0.5 to 2
- segments: int32 [8, 512], P('dp'), may hold values from 0 to 5, never falling along the last dimension, each value on 1 to 256 neighbouring positions
Outputs:
- ends_out: float32 [2, 8, 512, 1024], P('pipe', 'dp', 'tensor')
- mix_in_grad: float32 [2, 1024, 2, 1024], P('pipe', 'dp', None, 'tensor')
- mix_out_grad: float32 [2, 1024, 1024], P('pipe', 'tensor', 'dp')
- gate_up_grad: float32 [2, 1024, 2, 4608], P('pipe', 'dp', None, 'tensor')
- down_grad: float32 [2, 4608, 1024], P('pipe', 'tensor', 'dp')
- value_grad: float32 [1024, 1024], P(('pipe', 'dp'), 'tensor')
- gains_one_grad: float32 [2, 1024], replicated
- gains_two_grad: float32 [2, 1024], replicated
- conv_grad: float32 [3, 1024], replicated
- qk_grad: float32 [2, 64], replicated
The draws below stay inside these ranges and needn't reach their ends.
Inputs may be any that keep to these rules, and one draw needn't show every extreme that they name: `segments`: document numbers never fall along a sequence; each document is 1 to 256 tokens long and some document has exactly 256.
All inputs are finite; a program needn't handle non-finite values.
Results may differ from the reference program's by a relative error of at most 0.017.
The reference program's roundings to bfloat16 on the way count: a program that leaves them out, or rounds other values in their place, can miss the bound.
Values may be sent and summed in bfloat16 or wider, within the bound.
No kernel may reach another device: no remote copies, remote signals or barrier semaphores. Data moves between devices by JAX's collectives and lax.ppermute only.
A program may use at most 320 MiB of HBM per device.

```python
import math
import jax
import jax.numpy as jnp
import numpy as np
from jax import lax

D = 1024
FF = 4608
HEADS = 16
KV_HEADS = 8
HEAD_DIM = 64
SEQ_LEN = 512
SEQUENCES = 8


def block_scale(rng, shape, pieces, least, high):
    def one(dim, blocks):
        heights = jax.random.uniform(jax.random.fold_in(jax.random.fold_in(rng, 6), dim), (blocks,), jnp.float32, least / len(pieces), high / len(pieces))
        return jnp.repeat(jnp.exp(heights), shape[dim] // blocks).reshape((-1,) + (1,) * (len(shape) - dim - 1))

    level = one(*pieces[0])
    for cut in pieces[1:]:
        level = level * one(*cut)
    return level


def profile(number_of, total, limit, slope):
    portions = [(1 << 20) // math.isqrt(grade ** slope) + 1 for grade in range(2, number_of + 1)]
    surplus, counts = total - limit - (number_of - 1), [1] * (number_of - 1)
    while surplus > 0:
        movable = [i for i in range(number_of - 1) if counts[i] < limit]
        pool, budget = sum([portions[i] for i in movable]), surplus
        for i in movable:
            extra = min(limit - counts[i], max(1, budget * portions[i] // pool), surplus)
            counts[i] = counts[i] + extra
            surplus = surplus - extra
    return np.array([limit] + counts)


def uneven_parts(key, amount, total, most, lean):
    if amount == 2:
        one = jax.random.randint(key, (), max(1, total - most), min(most, total - 1) + 1)
        return jnp.stack([one, total - one])
    lengths = jnp.asarray(profile(amount, total, most, lean), jnp.int32)
    twos = (amount - 1) // 2
    source_of, taker = lengths[1:1 + 2 * twos:2], lengths[2:2 + 2 * twos:2]
    margin = jnp.minimum(source_of - 1, most - taker)
    moved = jax.random.randint(jax.random.fold_in(key, 1), (twos,), 0, 1 << 20) % (margin + 1)
    lengths = lengths.at[1:1 + 2 * twos:2].set(source_of - moved).at[2:2 + 2 * twos:2].set(taker + moved)
    return lengths[jax.random.permutation(jax.random.fold_in(key, 2), amount)]


def normal_values(stream_key, extent, width, most, pieces=(), kind=jnp.bfloat16):
    entries = jax.random.normal(stream_key, extent, jnp.float32) * width
    if len(pieces) > 0:
        entries = block_scale(stream_key, extent, pieces, -0.22, 0.18) * entries
    return jnp.clip(entries, min=-most, max=most).astype(kind)


def setup_inputs(seed: int = 0) -> dict:
    splits = jax.random.split(jax.random.key(seed), 12)
    return {
        "ends": normal_values(splits[0], (2, SEQUENCES, SEQ_LEN, D), 1.0, 6.0, ((0, 2), (1, 4), (2, 4)), jnp.float32),
        "mix_in": normal_values(splits[1], (2, D, 2, D), D ** -0.5, 0.1875, ((0, 2), (1, 4), (3, 4))),
        "mix_out": normal_values(splits[2], (2, D, D), (D // 16) ** -0.5, 0.75, ((0, 2), (1, 4), (2, 4))),
        "gate_up": normal_values(splits[3], (2, D, 2, FF), D ** -0.5, 0.1875, ((0, 2), (1, 4), (3, 4))),
        "down": normal_values(splits[4], (2, FF, D), FF ** -0.5, 0.09375, ((0, 2), (1, 4), (2, 4))),
        "value_weight": normal_values(splits[5], (D, D), D ** -0.5, 0.1875, ((0, 8), (1, 4))),
        "gains_one": jnp.clip(1.0 + 0.15 * jax.random.normal(splits[6], (2, D), jnp.float32), 0.25, 1.75),
        "gains_two": jnp.clip(1.0 + 0.15 * jax.random.normal(splits[7], (2, D), jnp.float32), 0.25, 1.75),
        "conv_kernel": jnp.clip(jax.random.uniform(splits[8], (3, D), jnp.float32, -1.0, 1.0), -1.0, 1.0),
        "qk_gains": jnp.clip(jnp.exp(jax.random.uniform(splits[9], (2, HEAD_DIM), jnp.float32, math.log(0.5), math.log(2.0))), 0.5, 2.0),
        "segments": jax.vmap(lambda own: jnp.searchsorted(jnp.cumsum(uneven_parts(own, 6, SEQ_LEN, SEQ_LEN // 2, 1)), jnp.arange(SEQ_LEN), side="right"))(jax.random.split(splits[10], SEQUENCES)).reshape((SEQUENCES, SEQ_LEN)).astype(jnp.int32),
    }


EPS = 1e-05
THETA = 1000000.0
NEG = -1e+30

def to_half(values):
    return values.astype(jnp.bfloat16)

def matmul(operand, partner):
    return jnp.dot(operand, partner, preferred_element_type=jnp.float32)

def outer_sum(operand, partner):
    return lax.dot_general(operand, partner, (((0,), (0,)), ((), ())), preferred_element_type=jnp.float32)

def back_product(operand, partner):
    return lax.dot_general(operand, partner, (((1,), (1,)), ((), ())), preferred_element_type=jnp.float32)

def norm_forward(values, gain):
    recip = lax.rsqrt(lax.optimization_barrier(jnp.mean(values * values, axis=-1, keepdims=True)) + EPS)
    normed = values * recip
    return (normed * gain, normed, recip)

def norm_backward(grad, normed, recip, gain):
    scaled = grad * gain
    back = recip * (scaled - normed * lax.optimization_barrier(jnp.mean(scaled * normed, axis=-1, keepdims=True)))
    return (back, lax.optimization_barrier(jnp.sum(grad * normed, axis=tuple(range(grad.ndim - 1)))))

def delay(values, steps):
    return jnp.pad(values, ((steps, 0), (0, 0)))[:values.shape[0]]

def advance(values, steps):
    return jnp.pad(values, ((0, steps), (0, 0)))[steps:]

def rope_tables(seg):
    index = jnp.arange(seg.shape[0], dtype=jnp.int32)
    change = jnp.concatenate([jnp.ones((1,), jnp.int32), (seg[1:] != seg[:-1]).astype(jnp.int32)])
    first = lax.cummax(jnp.where(change > 0, index, 0), axis=0)
    position = (index - first).astype(jnp.float32)
    freqs = THETA ** (-2.0 * jnp.arange(HEAD_DIM // 2, dtype=jnp.float32) / HEAD_DIM)
    angle = position[:, None] * freqs[None, :]
    return (jnp.cos(angle)[:, None, :], jnp.sin(angle)[:, None, :])

def rotate(values, cosine, sine):
    half = values.shape[-1] // 2
    first, second = (values[..., :half], values[..., half:])
    return jnp.concatenate([first * cosine - second * sine, second * cosine + first * sine], axis=-1)

def rotate_back(grad, cosine, sine):
    half = grad.shape[-1] // 2
    first, second = (grad[..., :half], grad[..., half:])
    return jnp.concatenate([first * cosine + second * sine, second * cosine - first * sine], axis=-1)

def ffn_forward(stream, gain, w_gu, w_dn):
    normed_out, normed, recip = norm_forward(stream, gain)
    inputs = to_half(normed_out)
    gate = matmul(inputs, w_gu[:, 0])
    upward = matmul(inputs, w_gu[:, 1])
    hidden = to_half(jax.nn.silu(gate) * upward)
    return (stream + matmul(hidden, w_dn), (normed, recip, inputs, gate, upward, hidden))

def ffn_backward(grad_out, gain, w_gu, w_dn, saved):
    normed, recip, inputs, gate, upward, hidden = saved
    grad_half = to_half(grad_out)
    grad_hidden = back_product(grad_half, w_dn)
    sigma = jax.nn.sigmoid(gate)
    grad_gate = to_half(grad_hidden * upward * sigma * (1.0 + gate * (1.0 - sigma)))
    grad_up = to_half(grad_hidden * gate * sigma)
    d_down = outer_sum(hidden, grad_half)
    d_gate_up = jnp.stack([outer_sum(inputs, grad_gate), outer_sum(inputs, grad_up)], axis=1)
    grad_in = back_product(grad_gate, w_gu[:, 0]) + back_product(grad_up, w_gu[:, 1])
    back, d_gain = norm_backward(grad_in, normed, recip, gain)
    return (grad_out + back, d_gate_up, d_down, d_gain)

def first_forward(stream, w_bc, w_val, w_out, w_gu, w_dn, gains, kernel):
    normed_out, normed, recip = norm_forward(stream, gains[0])
    inputs = to_half(normed_out)
    bgate = matmul(inputs, w_bc[:, 0])
    cgate = matmul(inputs, w_bc[:, 1])
    values = matmul(inputs, w_val)
    mixed = bgate * values
    convolved = kernel[2] * mixed + kernel[1] * delay(mixed, 1) + kernel[0] * delay(mixed, 2)
    gated = to_half(cgate * convolved)
    middle = stream + matmul(gated, w_out)
    out, ffn_saved = ffn_forward(middle, gains[1], w_gu, w_dn)
    return (out, (normed, recip, inputs, bgate, cgate, values, mixed, convolved, gated, ffn_saved))

def first_backward(grad_out, saved, w_bc, w_val, w_out, w_gu, w_dn, gains, kernel):
    normed, recip, inputs, bgate, cgate, values, mixed, convolved, gated, ffn_saved = saved
    grad_mid, d_gate_up, d_down, d_gain_two = ffn_backward(grad_out, gains[1], w_gu, w_dn, ffn_saved)
    grad_half = to_half(grad_mid)
    grad_gated = back_product(grad_half, w_out)
    d_out = outer_sum(gated, grad_half)
    grad_conv = grad_gated * cgate
    grad_c = to_half(grad_gated * convolved)
    grad_mixed = kernel[2] * grad_conv + kernel[1] * advance(grad_conv, 1) + kernel[0] * advance(grad_conv, 2)
    d_kernel = jnp.stack([lax.optimization_barrier(jnp.sum(grad_conv * delay(mixed, 2), axis=0)), lax.optimization_barrier(jnp.sum(grad_conv * delay(mixed, 1), axis=0)), lax.optimization_barrier(jnp.sum(grad_conv * mixed, axis=0))])
    grad_b = to_half(grad_mixed * values)
    grad_v = to_half(grad_mixed * bgate)
    d_bc = jnp.stack([outer_sum(inputs, grad_b), outer_sum(inputs, grad_c)], axis=1)
    d_val = outer_sum(inputs, grad_v)
    grad_in = back_product(grad_b, w_bc[:, 0]) + back_product(grad_c, w_bc[:, 1]) + back_product(grad_v, w_val)
    back, d_gain_one = norm_backward(grad_in, normed, recip, gains[0])
    return (grad_mid + back, (d_bc, d_out, d_gate_up, d_down, d_val, jnp.stack([d_gain_one, d_gain_two]), d_kernel))

def second_block(stream, grad_out, seg, w_qkv, w_out, w_gu, w_dn, gains, qk_gains):
    length = stream.shape[0]
    group = HEADS // KV_HEADS
    scale = 1.0 / HEAD_DIM ** 0.5
    normed_out, normed, recip = norm_forward(stream, gains[0])
    inputs = to_half(normed_out)
    query = matmul(inputs, w_qkv[:, 0]).reshape(length, HEADS, HEAD_DIM)
    paired = matmul(inputs, w_qkv[:, 1]).reshape(length, KV_HEADS, 2, HEAD_DIM)
    q_out, q_norm, q_recip = norm_forward(query, qk_gains[0])
    k_out, k_norm, k_recip = norm_forward(paired[:, :, 0], qk_gains[1])
    cosine, sine = rope_tables(seg)
    q_half = to_half(rotate(q_out, cosine, sine)).reshape(length, KV_HEADS, group, HEAD_DIM)
    k_half = to_half(rotate(k_out, cosine, sine))
    v_half = to_half(paired[:, :, 1])
    index = jnp.arange(length, dtype=jnp.int32)
    allowed = (seg[:, None] == seg[None, :]) & (index[None, :] <= index[:, None])
    scores = jnp.einsum('angd,bnd->ngab', q_half.astype(jnp.float32), k_half.astype(jnp.float32)) * scale
    masked = jnp.where(allowed[None, None], scores, NEG)
    top = lax.optimization_barrier(jnp.max(masked, axis=-1, keepdims=True))
    lse = top + jnp.log(lax.optimization_barrier(jnp.sum(jnp.exp(masked - top), axis=-1, keepdims=True)))
    prob = jnp.exp(masked - lse)
    p_half = to_half(prob)
    attended = jnp.einsum('ngab,bnd->angd', p_half.astype(jnp.float32), v_half.astype(jnp.float32))
    a_half = to_half(attended.reshape(length, HEADS * HEAD_DIM))
    middle = stream + matmul(a_half, w_out)
    out, ffn_saved = ffn_forward(middle, gains[1], w_gu, w_dn)
    grad_mid, d_gate_up, d_down, d_gain_two = ffn_backward(grad_out, gains[1], w_gu, w_dn, ffn_saved)
    grad_half = to_half(grad_mid)
    grad_attn = to_half(back_product(grad_half, w_out)).reshape(length, KV_HEADS, group, HEAD_DIM)
    d_out = outer_sum(a_half, grad_half)
    grad_prob = jnp.einsum('angd,bnd->ngab', grad_attn.astype(jnp.float32), v_half.astype(jnp.float32))
    delta = lax.optimization_barrier(jnp.sum(prob * grad_prob, axis=-1, keepdims=True))
    grad_score = to_half(prob * (grad_prob - delta)).astype(jnp.float32)
    grad_v = jnp.einsum('ngab,angd->bnd', p_half.astype(jnp.float32), grad_attn.astype(jnp.float32))
    grad_q = jnp.einsum('ngab,bnd->angd', grad_score, k_half.astype(jnp.float32)) * scale
    grad_k = jnp.einsum('ngab,angd->bnd', grad_score, q_half.astype(jnp.float32)) * scale
    grad_q = rotate_back(grad_q.reshape(length, HEADS, HEAD_DIM), cosine, sine)
    grad_k = rotate_back(grad_k, cosine, sine)
    grad_q, d_qgain = norm_backward(grad_q, q_norm, q_recip, qk_gains[0])
    grad_k, d_kgain = norm_backward(grad_k, k_norm, k_recip, qk_gains[1])
    q_grad_half = to_half(grad_q).reshape(length, HEADS * HEAD_DIM)
    pair_half = to_half(jnp.stack([grad_k, grad_v], axis=2)).reshape(length, 2 * KV_HEADS * HEAD_DIM)
    d_qkv = jnp.stack([outer_sum(inputs, q_grad_half), outer_sum(inputs, pair_half)], axis=1)
    grad_in = back_product(q_grad_half, w_qkv[:, 0]) + back_product(pair_half, w_qkv[:, 1])
    back, d_gain_one = norm_backward(grad_in, normed, recip, gains[0])
    grads = (d_qkv, d_out, d_gate_up, d_down, jnp.stack([d_gain_one, d_gain_two]), jnp.stack([d_qgain, d_kgain]))
    return (out, grad_mid + back, grads)

def reference(ends, mix_in, mix_out, gate_up, down, value_weight, gains_one, gains_two, conv_kernel, qk_gains, segments):
    first_kit = (mix_in[0], value_weight, mix_out[0], gate_up[0], down[0], gains_one, conv_kernel)
    second_kit = (mix_in[1], mix_out[1], gate_up[1], down[1], gains_two, qk_gains)

    def one_sequence(carry, items):
        stream, grad_out, seg = items
        middle, saved = first_forward(stream, *first_kit)
        out, grad_mid, second_grads = second_block(middle, grad_out, seg, *second_kit)
        grad_in, first_grads = first_backward(grad_mid, saved, *first_kit)
        carry = jax.tree.map(jnp.add, carry, (first_grads, second_grads))
        return (carry, (grad_in, out))
    first_zero = (jnp.zeros((D, 2, D), jnp.float32), jnp.zeros((D, D), jnp.float32), jnp.zeros((D, 2, FF), jnp.float32), jnp.zeros((FF, D), jnp.float32), jnp.zeros((D, D), jnp.float32), jnp.zeros((2, D), jnp.float32), jnp.zeros((3, D), jnp.float32))
    second_zero = (jnp.zeros((D, 2, D), jnp.float32), jnp.zeros((D, D), jnp.float32), jnp.zeros((D, 2, FF), jnp.float32), jnp.zeros((FF, D), jnp.float32), jnp.zeros((2, D), jnp.float32), jnp.zeros((2, HEAD_DIM), jnp.float32))
    totals, (grad_in, out) = lax.scan(one_sequence, (first_zero, second_zero), (ends[0], ends[1], segments))
    first_grads, second_grads = totals
    ends_out = jnp.stack([grad_in, out])
    mix_in_grad = jnp.stack([first_grads[0], second_grads[0]])
    mix_out_grad = jnp.stack([first_grads[1], second_grads[1]])
    gate_up_grad = jnp.stack([first_grads[2], second_grads[2]])
    down_grad = jnp.stack([first_grads[3], second_grads[3]])
    return (ends_out, mix_in_grad, mix_out_grad, gate_up_grad, down_grad, first_grads[4], first_grads[5], second_grads[4], first_grads[6], second_grads[5])
```

```python
import jax
import jax.numpy as jnp
from jax import lax
from jax.sharding import PartitionSpec as P

EPS = 1e-05
THETA = 1000000.0
NEG = -1e30
LONGEST = 256


BF = jnp.bfloat16
F32 = jnp.float32


def dot(a, b):
    return jnp.dot(a, b, preferred_element_type=F32)


def dot_tn(a, b):
    return lax.dot_general(a, b, (((0,), (0,)), ((), ())), preferred_element_type=F32)


def dot_nt(a, b):
    return lax.dot_general(a, b, (((1,), (1,)), ((), ())), preferred_element_type=F32)


def by_xor(value, axis, mask):
    size = lax.axis_size(axis)
    return lax.ppermute(value, axis, [(i, i ^ mask) for i in range(size)])


def by_shift(value, axis, by):
    size = lax.axis_size(axis)
    pairs = [(i, i + by) for i in range(size) if 0 <= i + by < size]
    return lax.ppermute(value, axis, pairs)


def others(axis):
    return range(1, lax.axis_size(axis))


def xor_list(items, index):
    bit = 1
    while bit < len(items):
        on = (index & bit) != 0
        items = [jnp.where(on, items[i ^ bit], items[i]) for i in range(len(items))]
        bit *= 2
    return items


def cut(value, count, axis=-1):
    return jnp.split(value, count, axis=axis)


class Order:
    def __init__(self):
        self.pipe = lax.axis_index("pipe")
        self.dp = lax.axis_index("dp")
        self.tensor = lax.axis_index("tensor")
        self.n_pipe = lax.axis_size("pipe")
        self.n_dp = lax.axis_size("dp")
        self.n_tensor = lax.axis_size("tensor")

    def to_local(self, value):
        pieces = cut(value, self.n_dp * self.n_pipe)
        pieces = xor_list(pieces, self.dp * self.n_pipe + self.pipe)
        moved = [pieces[s * self.n_pipe + q] for q in range(self.n_pipe) for s in range(self.n_dp)]
        return jnp.concatenate(moved, axis=-1)

    def to_true(self, value):
        pieces = cut(value, self.n_dp * self.n_pipe)
        moved = [pieces[q * self.n_dp + s] for s in range(self.n_dp) for q in range(self.n_pipe)]
        return jnp.concatenate(
            xor_list(moved, self.dp * self.n_pipe + self.pipe), axis=-1
        )

    def z_columns(self, value):
        return jnp.concatenate(xor_list(cut(value, self.n_tensor), self.tensor), axis=-1)


def norm_forward(values, gain):
    recip = lax.rsqrt(jnp.mean(values * values, axis=-1, keepdims=True) + EPS)
    normed = values * recip
    return (normed * gain, normed, recip)


def norm_backward(grad, normed, recip, gain):
    scaled = grad * gain
    back = recip * (scaled - normed * jnp.mean(scaled * normed, axis=-1, keepdims=True))
    return (back, jnp.sum(grad * normed, axis=tuple(range(grad.ndim - 1))))


def z_gather(rows):
    return [rows] + [by_xor(rows, "tensor", s) for s in others("tensor")]


def z_scatter(parts):
    moved = [by_xor(parts[s].astype(BF), "tensor", s) for s in others("tensor")]
    total = parts[0]
    for piece in moved:
        total = total + piece.astype(F32)
    return total


def dp_gather(half):
    mine = [half] + [by_xor(half, "dp", s) for s in others("dp")]
    theirs = [by_xor(piece, "pipe", 1) for piece in mine]
    return jnp.concatenate(mine + theirs, axis=0)


def dp_scatter(grad):
    size = grad.shape[0] // 2
    sent = grad[size:].astype(BF)
    total = grad[:size].astype(F32) + by_xor(sent, "pipe", 1).astype(F32)
    rows = size // lax.axis_size("dp")
    moved = [
        by_xor(total[s * rows : (s + 1) * rows].astype(BF), "dp", s) for s in others("dp")
    ]
    result = total[:rows]
    for piece in moved:
        result = result + piece.astype(F32)
    return result


def all_sum(value):
    for axis in ("pipe", "dp", "tensor"):
        bit = 1
        while bit < lax.axis_size(axis):
            value = value + by_xor(value, axis, bit)
            bit *= 2
    return value


def delay(values, steps):
    return jnp.pad(values, ((0, 0), (steps, 0), (0, 0)))[:, : values.shape[1]]


def advance(values, steps):
    return jnp.pad(values, ((0, 0), (0, steps), (0, 0)))[:, steps:]


def rotate(values, cosine, sine):
    half = values.shape[-1] // 2
    first, second = (values[..., :half], values[..., half:])
    return jnp.concatenate(
        [first * cosine - second * sine, second * cosine + first * sine], axis=-1
    )


def rotate_back(grad, cosine, sine):
    half = grad.shape[-1] // 2
    first, second = (grad[..., :half], grad[..., half:])
    return jnp.concatenate(
        [first * cosine + second * sine, second * cosine - first * sine], axis=-1
    )


def per_device(
    ends,
    mix_in,
    mix_out,
    gate_up,
    down,
    value_weight,
    gains_one,
    gains_two,
    conv_kernel,
    qk_gains,
    segments,
):
    order = Order()
    pipe, dp, tensor = order.pipe, order.dp, order.tensor
    n_pipe, n_dp, n_tensor = order.n_pipe, order.n_dp, order.n_tensor
    first = pipe == 0

    stream = ends[0]
    all_count, quarter, width = stream.shape
    count = all_count // n_pipe
    rows = count * quarter
    length = segments.shape[1]
    channels = mix_in.shape[3]
    hidden = gate_up.shape[3]
    head_size = qk_gains.shape[1]
    full = channels * n_tensor
    heads = full // head_size
    kv_heads = heads // 2
    group = heads // kv_heads
    scale = 1.0 / head_size**0.5

    kept = jnp.where(first, stream[:count], stream[count:])
    given = jnp.where(first, stream[count:], stream[:count])
    came = by_xor(given, "pipe", 1)
    h0 = order.to_local(jnp.where(first, kept, came).reshape(rows, width))
    cot = order.to_local(jnp.where(first, came, kept).reshape(rows, width))
    g_one = order.to_local(gains_one)
    g_two = order.to_local(gains_two)
    seg = jnp.where(first, segments[:count], segments[count:])

    def halves(raw):
        size = raw.shape[0] // 2
        low, high = raw[:size], raw[size:]
        mine = jnp.where(first, low, high)
        recv = by_xor(jnp.where(first, high, low), "pipe", 1)
        return (jnp.where(first, mine, recv), jnp.where(first, recv, mine))

    in_one, in_two = halves(jnp.concatenate([mix_in[0, :, 0], mix_in[0, :, 1]], axis=1))
    out_one, out_two = halves(mix_out[0].T)
    ffn_one, ffn_two = halves(
        jnp.concatenate([gate_up[0, :, 0], gate_up[0, :, 1], down[0].T], axis=1)
    )
    value_pairs = []
    for a in range(n_pipe):
        for b in range(n_dp):
            k = b * n_pipe + a
            value_pairs.append((k, a * n_dp + b))
    value_half = lax.ppermute(value_weight, ("pipe", "dp"), value_pairs)

    w_bcx = dp_gather(jnp.concatenate([in_one, value_half], axis=1))
    w_out1 = dp_gather(jnp.concatenate(z_gather(out_one), axis=1))
    w_ffn1 = dp_gather(ffn_one)
    q_part = [piece for piece in z_gather(in_two)]
    w_two = dp_gather(
        jnp.concatenate(
            [piece[:, :channels] for piece in q_part]
            + [piece[:, channels:] for piece in q_part]
            + z_gather(out_two),
            axis=1,
        )
    )
    w_ffn2 = dp_gather(ffn_two)
    w_qkv, w_out2 = w_two[:, : 2 * full], w_two[:, 2 * full :]

    cot_half = cot.astype(BF)
    cot_rows = jnp.concatenate(z_gather(cot_half), axis=0)

    a1, n1, r1 = norm_forward(h0, g_one[0])
    a1_list = z_gather(a1.astype(BF).reshape(count, quarter, width))
    a1_rows = jnp.concatenate(xor_list(a1_list, tensor), axis=1).reshape(count * length, width)
    kernel = lax.dynamic_slice_in_dim(conv_kernel, tensor * channels, channels, 1)
    bcx = dot(a1_rows, w_bcx).reshape(count, length, 3 * channels)
    bgate, cgate, values = cut(bcx, 3)
    mixed = bgate * values
    convolved = kernel[2] * mixed + kernel[1] * delay(mixed, 1) + kernel[0] * delay(mixed, 2)
    gated = (cgate * convolved).astype(BF)
    y_list = xor_list(cut(gated, n_tensor, 1), tensor)
    y_list = [y_list[0]] + [by_xor(y_list[s], "tensor", s) for s in others("tensor")]
    y_full = jnp.concatenate(y_list, axis=-1).reshape(rows, full)
    h1 = h0 + dot_nt(y_full, w_out1)

    def ffn_parts(w):
        return (w[:, :hidden], w[:, hidden : 2 * hidden], w[:, 2 * hidden :])

    a2, n2, r2 = norm_forward(h1, g_one[1])
    a2_rows = jnp.concatenate(z_gather(a2.astype(BF)), axis=0)
    wg1, wu1, wd1 = ffn_parts(w_ffn1)
    gate1 = dot(a2_rows, wg1)
    up1 = dot(a2_rows, wu1)
    z1 = (jax.nn.silu(gate1) * up1).astype(BF)
    out1 = h1 + z_scatter(cut(dot_nt(z1, wd1), n_tensor, 0))

    a3, n3, r3 = norm_forward(out1, g_two[0])
    a3_half = a3.astype(BF)
    qkv = dot(a3_half, w_qkv)
    query = order.z_columns(qkv[:, :full]).reshape(count, quarter, heads, head_size)
    paired = order.z_columns(qkv[:, full:]).reshape(count, quarter, kv_heads, 2, head_size)
    q_out, q_norm, q_recip = norm_forward(query, qk_gains[0])
    k_out, k_norm, k_recip = norm_forward(paired[:, :, :, 0], qk_gains[1])
    start = tensor * quarter
    seg_own = lax.dynamic_slice_in_dim(seg, start, quarter, 1)
    before = jnp.sum((seg[:, None, :] < seg_own[:, :, None]).astype(jnp.int32), axis=-1)
    index = start + lax.broadcasted_iota(jnp.int32, (count, quarter), 1)
    position = (index - before).astype(F32)
    freqs = THETA ** (-2.0 * jnp.arange(head_size // 2, dtype=F32) / head_size)
    angle = position[:, :, None] * freqs
    cosine, sine = jnp.cos(angle)[:, :, None, :], jnp.sin(angle)[:, :, None, :]
    q_half = rotate(q_out, cosine, sine).astype(BF).reshape(
        count, quarter, kv_heads, group, head_size
    )
    k_half = rotate(k_out, cosine, sine).astype(BF)
    v_half = paired[:, :, :, 1].astype(BF)
    reach = min(-(-(LONGEST - 1) // quarter), n_tensor - 1)
    kv_own = jnp.stack([k_half, v_half])
    kv_parts = [by_shift(kv_own, "tensor", j) for j in range(reach, 0, -1)] + [kv_own]
    kv = jnp.concatenate(kv_parts, axis=2)
    keys, vals = kv[0], kv[1]
    span = (reach + 1) * quarter
    seg_keys = lax.dynamic_slice_in_dim(
        jnp.pad(seg, ((0, 0), (reach * quarter, 0)), constant_values=-1), start, span, 1
    )
    row_at = lax.broadcasted_iota(jnp.int32, (quarter, span), 0) + reach * quarter
    col_at = lax.broadcasted_iota(jnp.int32, (quarter, span), 1)
    allowed = (seg_own[:, :, None] == seg_keys[:, None, :]) & (col_at <= row_at)[None]
    scores = (
        jnp.einsum("sangd,sbnd->sngab", q_half, keys, preferred_element_type=F32) * scale
    )
    masked = jnp.where(allowed[:, None, None], scores, NEG)
    highest = jnp.max(masked, axis=-1, keepdims=True)
    lse = highest + jnp.log(jnp.sum(jnp.exp(masked - highest), axis=-1, keepdims=True))
    prob = jnp.exp(masked - lse)
    p_half = prob.astype(BF)
    attended = jnp.einsum("sngab,sbnd->sangd", p_half, vals, preferred_element_type=F32)
    o_local = order.z_columns(attended.astype(BF).reshape(rows, full))
    h3 = out1 + dot_nt(o_local, w_out2)

    a4, n4, r4 = norm_forward(h3, g_two[1])
    a4_rows = jnp.concatenate(z_gather(a4.astype(BF)), axis=0)

    def ffn_backward(a_rows, gate, up, zed, c_rows, w):
        wg, wu, wd = ffn_parts(w)
        grad_hidden = dot(c_rows, wd)
        sigma = jax.nn.sigmoid(gate)
        grad_gate = (grad_hidden * up * sigma * (1.0 + gate * (1.0 - sigma))).astype(BF)
        grad_up = (grad_hidden * gate * sigma).astype(BF)
        back = dot_nt(grad_gate, wg) + dot_nt(grad_up, wu)
        d_w = jnp.concatenate(
            [
                dot_tn(a_rows, grad_gate).astype(BF),
                dot_tn(a_rows, grad_up).astype(BF),
                dot_tn(c_rows, zed).astype(BF),
            ],
            axis=1,
        )
        return (z_scatter(cut(back, n_tensor, 0)), d_w)

    wg2, wu2, wd2 = ffn_parts(w_ffn2)
    gate2 = dot(a4_rows, wg2)
    up2 = dot(a4_rows, wu2)
    z2 = (jax.nn.silu(gate2) * up2).astype(BF)
    da4, d_ffn2 = ffn_backward(a4_rows, gate2, up2, z2, cot_rows, w_ffn2)
    out2 = h3 + z_scatter(cut(dot_nt(z2, wd2), n_tensor, 0))
    back4, d_gain4 = norm_backward(da4, n4, r4, g_two[1])
    dh3 = cot + back4

    db3 = dh3.astype(BF)
    do_half = order.z_columns(dot(db3, w_out2).astype(BF))
    do_half = do_half.reshape(count, quarter, kv_heads, group, head_size)
    d_out2 = dot_tn(db3, o_local).astype(BF)
    grad_prob = jnp.einsum("sangd,sbnd->sngab", do_half, vals, preferred_element_type=F32)
    delta = jnp.sum(prob * grad_prob, axis=-1, keepdims=True)
    ds = (prob * (grad_prob - delta)).astype(BF)
    dv = jnp.einsum("sngab,sangd->sbnd", p_half, do_half, preferred_element_type=F32)
    dq = jnp.einsum("sngab,sbnd->sangd", ds, keys, preferred_element_type=F32) * scale
    dk = jnp.einsum("sngab,sangd->sbnd", ds, q_half, preferred_element_type=F32) * scale
    dkv = jnp.stack([dk, dv])
    total = dkv[:, :, reach * quarter :]
    for j in range(1, reach + 1):
        part = dkv[:, :, (reach - j) * quarter : (reach - j + 1) * quarter].astype(BF)
        total = total + by_shift(part, "tensor", -j).astype(F32)
    dq = rotate_back(dq.reshape(count, quarter, heads, head_size), cosine, sine)
    dk = rotate_back(total[0], cosine, sine)
    dq, d_qgain = norm_backward(dq, q_norm, q_recip, qk_gains[0])
    dk, d_kgain = norm_backward(dk, k_norm, k_recip, qk_gains[1])
    dq = order.z_columns(dq.astype(BF).reshape(rows, full))
    dkv = order.z_columns(jnp.stack([dk, total[1]], axis=3).astype(BF).reshape(rows, full))
    dqkv = jnp.concatenate([dq, dkv], axis=1)
    d_two = jnp.concatenate([dot_tn(a3_half, dqkv).astype(BF), d_out2], axis=1)
    back3, d_gain3 = norm_backward(dot_nt(dqkv, w_qkv), n3, r3, g_two[0])
    dout1 = dh3 + back3

    c1_rows = jnp.concatenate(z_gather(dout1.astype(BF)), axis=0)
    da2, d_ffn1 = ffn_backward(a2_rows, gate1, up1, z1, c1_rows, w_ffn1)
    back2, d_gain2 = norm_backward(da2, n2, r2, g_one[1])
    dh1 = dout1 + back2

    db1 = dh1.astype(BF)
    dy_list = cut(dot(db1, w_out1).astype(BF).reshape(count, quarter, full), n_tensor)
    dy_list = [dy_list[0]] + [by_xor(dy_list[s], "tensor", s) for s in others("tensor")]
    dy = jnp.concatenate(xor_list(dy_list, tensor), axis=1).astype(F32)
    d_out1 = dot_tn(db1, y_full).astype(BF)
    du = dy * cgate
    dc = (dy * convolved).astype(BF)
    dm = kernel[2] * du + kernel[1] * advance(du, 1) + kernel[0] * advance(du, 2)
    d_kernel = jnp.stack(
        [
            jnp.sum(du * delay(mixed, 2), axis=(0, 1)),
            jnp.sum(du * delay(mixed, 1), axis=(0, 1)),
            jnp.sum(du * mixed, axis=(0, 1)),
        ]
    )
    dbcx = jnp.concatenate([(dm * values).astype(BF), dc, (dm * bgate).astype(BF)], axis=-1)
    dbcx_rows = dbcx.reshape(count * length, 3 * channels)
    d_bcx = dot_tn(a1_rows, dbcx_rows).astype(BF)
    da1 = dot_nt(dbcx_rows, w_bcx).reshape(count, length, width)
    da1 = z_scatter(xor_list(cut(da1, n_tensor, 1), tensor)).reshape(rows, width)
    back1, d_gain1 = norm_backward(da1, n1, r1, g_one[0])
    dh0 = dh1 + back1

    def z_sum(grad):
        return z_scatter(cut(grad, n_tensor))

    r_ffn2 = dp_scatter(d_ffn2)
    r_two = dp_scatter(d_two)
    r_q, r_kv, r_out2 = cut(r_two, 3)
    r_q, r_kv, r_out2 = z_sum(r_q), z_sum(r_kv), z_sum(r_out2)
    r_ffn1 = dp_scatter(d_ffn1)
    r_out1 = z_sum(dp_scatter(d_out1))
    r_bcx = dp_scatter(d_bcx)
    r_b, r_c, r_x = cut(r_bcx, 3)

    def whole(one, two):
        recv = by_xor(jnp.where(first, two, one), "pipe", 1)
        mine = jnp.where(first, one, two)
        return jnp.concatenate(
            [jnp.where(first, mine, recv), jnp.where(first, recv, mine)], axis=0
        )

    g_ffn = whole(r_ffn1, r_ffn2)
    g_mix = whole(
        jnp.concatenate([r_b, r_c, r_out1], axis=1), jnp.concatenate([r_q, r_kv, r_out2], axis=1)
    )
    mix_in_grad = jnp.stack([g_mix[:, :channels], g_mix[:, channels : 2 * channels]], axis=1)
    mix_out_grad = g_mix[:, 2 * channels :].T
    gate_up_grad = jnp.stack([g_ffn[:, :hidden], g_ffn[:, hidden : 2 * hidden]], axis=1)
    down_grad = g_ffn[:, 2 * hidden :].T
    value_grad = lax.ppermute(r_x, ("pipe", "dp"), [(b, a) for a, b in value_pairs])

    kernel_full = lax.dynamic_update_slice_in_dim(
        jnp.zeros(conv_kernel.shape, F32), d_kernel, tensor * channels, 1
    )
    gain_rows = order.to_true(jnp.stack([d_gain1, d_gain2, d_gain3, d_gain4]))
    qk_row = jnp.concatenate([d_qgain, d_kgain])[None]
    qk_row = jnp.pad(qk_row, ((0, 0), (0, width - qk_row.shape[1])))
    sums = all_sum(jnp.concatenate([gain_rows, kernel_full, qk_row], axis=0))
    taps = conv_kernel.shape[0]
    sum_kernel = sums[4 : 4 + taps]
    sum_qk = sums[4 + taps, : 2 * head_size].reshape(2, head_size)

    dh0 = order.to_true(dh0).reshape(count, quarter, width)
    out2 = order.to_true(out2).reshape(count, quarter, width)
    recv = by_xor(jnp.where(first, out2, dh0), "pipe", 1)
    ends_out = jnp.concatenate(
        [jnp.where(first, dh0, recv), jnp.where(first, recv, out2)], axis=0
    )
    return (
        ends_out[None],
        mix_in_grad[None],
        mix_out_grad[None],
        gate_up_grad[None],
        down_grad[None],
        value_grad,
        sums[0:2],
        sums[2:4],
        sum_kernel,
        sum_qk,
    )


def solution(mesh):
    return jax.shard_map(
        per_device,
        mesh=mesh,
        in_specs=(
            P("pipe", "dp", "tensor", None),
            P("pipe", "dp", None, "tensor"),
            P("pipe", "tensor", "dp"),
            P("pipe", "dp", None, "tensor"),
            P("pipe", "tensor", "dp"),
            P(("pipe", "dp"), "tensor"),
            P(),
            P(),
            P(),
            P(),
            P("dp", None),
        ),
        out_specs=(
            P("pipe", "dp", "tensor", None),
            P("pipe", "dp", None, "tensor"),
            P("pipe", "tensor", "dp"),
            P("pipe", "dp", None, "tensor"),
            P("pipe", "tensor", "dp"),
            P(("pipe", "dp"), "tensor"),
            P(),
            P(),
            P(),
            P(),
        ),
        check_vma=False,
    )
```

```python
import jax
import jax.numpy as jnp
from jax import lax
from jax.experimental import pallas as pl
from jax.experimental.pallas import tpu as pltpu
from jax.sharding import PartitionSpec as P


EPS = 1e-05
THETA = 1000000.0
NEG = -1e30
LONGEST = 256


PIPE, DP, TENSOR = "pipe", "dp", "tensor"
BF = jnp.bfloat16
F32 = jnp.float32


def dot(a, b):
    return jnp.dot(a, b, preferred_element_type=F32)


def dot_tn(a, b):
    return lax.dot_general(a, b, (((0,), (0,)), ((), ())), preferred_element_type=F32)


def dot_nt(a, b):
    return lax.dot_general(a, b, (((1,), (1,)), ((), ())), preferred_element_type=F32)


def by_xor(value, axis, mask):
    size = lax.axis_size(axis)
    return lax.ppermute(value, axis, [(i, i ^ mask) for i in range(size)])


def by_shift(value, axis, by):
    size = lax.axis_size(axis)
    pairs = [(i, i + by) for i in range(size) if 0 <= i + by < size]
    return lax.ppermute(value, axis, pairs)


def others(axis):
    return range(1, lax.axis_size(axis))


def xor_list(items, index):
    bit = 1
    while bit < len(items):
        on = (index & bit) != 0
        items = [jnp.where(on, items[i ^ bit], items[i]) for i in range(len(items))]
        bit *= 2
    return items


def cut(value, count, axis=-1):
    return jnp.split(value, count, axis=axis)


class Order:
    def __init__(self):
        self.pipe = lax.axis_index(PIPE)
        self.dp = lax.axis_index(DP)
        self.tensor = lax.axis_index(TENSOR)
        self.n_pipe = lax.axis_size(PIPE)
        self.n_dp = lax.axis_size(DP)
        self.n_tensor = lax.axis_size(TENSOR)

    def to_local(self, value):
        pieces = cut(value, self.n_dp * self.n_pipe)
        moved = [pieces[c * self.n_pipe + q] for q in range(self.n_pipe) for c in range(self.n_dp)]
        return jnp.concatenate(moved, axis=-1)

    def to_true(self, value):
        pieces = cut(value, self.n_dp * self.n_pipe)
        moved = [pieces[q * self.n_dp + c] for c in range(self.n_dp) for q in range(self.n_pipe)]
        return jnp.concatenate(moved, axis=-1)


def norm_forward(values, gain):
    recip = lax.rsqrt(jnp.mean(values * values, axis=-1, keepdims=True) + EPS)
    normed = values * recip
    return (normed * gain, normed, recip)


def norm_backward(grad, normed, recip, gain):
    scaled = grad * gain
    back = recip * (scaled - normed * jnp.mean(scaled * normed, axis=-1, keepdims=True))
    return (back, jnp.sum(grad * normed, axis=tuple(range(grad.ndim - 1))))


def add_all(stream, pieces, n_pipe, n_dp):
    rows, width = stream.shape
    size = width // (n_pipe * n_dp)

    def body(*refs):
        for q in range(n_pipe):
            for c in range(n_dp):
                local = pl.ds((q * n_dp + c) * size, size)
                total = refs[0][:, local]
                for ref in refs[1:-1]:
                    total = total + ref[:, local].astype(F32)
                refs[-1][:, pl.ds((c * n_pipe + q) * size, size)] = total

    return pl.pallas_call(body, out_shape=jax.ShapeDtypeStruct((rows, width), F32))(
        stream, *pieces
    )


def assemble(pieces, index):
    count = len(pieces)
    height, width = pieces[0].shape

    def body(index_ref, *refs):
        for i in range(count):
            at = jnp.bitwise_xor(index_ref[0], i) * height
            refs[-1][pl.ds(pl.multiple_of(at, height), height), :] = refs[i][...]

    whole = pl.BlockSpec(memory_space=pltpu.MemorySpace.VMEM)
    return pl.pallas_call(
        body,
        out_shape=jax.ShapeDtypeStruct((count * height, width), pieces[0].dtype),
        in_specs=[pl.BlockSpec(memory_space=pltpu.MemorySpace.SMEM)] + [whole] * count,
        out_specs=whole,
    )(index.reshape(1).astype(jnp.int32), *pieces)


def xor_gather(half, dp):
    pieces = [half] + [by_xor(half, DP, s) for s in others(DP)]
    mine = assemble(pieces, dp)
    return (mine, by_xor(mine, PIPE, 1))


def z_gather(rows):
    return [rows] + [by_xor(rows, TENSOR, s) for s in others(TENSOR)]


def z_scatter(parts):
    moved = [by_xor(parts[s].astype(BF), TENSOR, s) for s in others(TENSOR)]
    total = parts[0].astype(F32)
    for piece in moved:
        total = total + piece.astype(F32)
    return total


def dp_gather(half):
    return lax.all_gather(half, (PIPE, DP), axis=0, tiled=True)


def by_half(value, first):
    low, high = cut(value, 2)
    return (jnp.where(first, low, high), jnp.where(first, high, low))


def pair_grad(lefts, rights, first):
    halves = [left if isinstance(left, tuple) else by_half(left, first) for left in lefts]
    sent = []
    for (_, left), right in zip(halves, rights, strict=True):
        sent.append(dot_tn(left, right).astype(BF))
    came = [by_xor(piece, PIPE, 1) for piece in sent]
    sums = [
        (dot_tn(left, right) + piece.astype(F32)).astype(BF)
        for (left, _), right, piece in zip(halves, rights, came, strict=True)
    ]
    return sums[0] if len(sums) == 1 else jnp.concatenate(sums, axis=1)


def dp_scatter(total):
    return lax.psum_scatter(total, DP, scatter_dimension=0, tiled=True).astype(F32)


def xor_scatter(total, dp):
    size = total.shape[0] // lax.axis_size(DP)
    pieces = [
        lax.dynamic_slice_in_dim(total, (dp ^ s) * size, size, 0)
        for s in range(lax.axis_size(DP))
    ]
    moved = [by_xor(pieces[s], DP, s) for s in others(DP)]
    result = pieces[0].astype(F32)
    for piece in moved:
        result = result + piece.astype(F32)
    return result


def all_sum(value):
    for axis in (PIPE, DP, TENSOR):
        sums = [value] + [by_xor(value, axis, s) for s in others(axis)]
        while len(sums) > 1:
            sums = [sums[i] + sums[i + 1] for i in range(0, len(sums), 2)]
        value = sums[0]
    return value


def delay(values, steps):
    return jnp.pad(values, ((0, 0), (steps, 0), (0, 0)))[:, : values.shape[1]]


def advance(values, steps):
    return jnp.pad(values, ((0, 0), (0, steps), (0, 0)))[:, steps:]


def rotate(values, cosine, sine):
    half = values.shape[-1] // 2
    first, second = (values[..., :half], values[..., half:])
    return jnp.concatenate(
        [first * cosine - second * sine, second * cosine + first * sine], axis=-1
    )


def rotate_back(grad, cosine, sine):
    half = grad.shape[-1] // 2
    first, second = (grad[..., :half], grad[..., half:])
    return jnp.concatenate(
        [first * cosine + second * sine, second * cosine - first * sine], axis=-1
    )


def compute(
    ends,
    mix_in,
    mix_out,
    gate_up,
    down,
    value_weight,
    gains_one,
    gains_two,
    conv_kernel,
    qk_gains,
    segments,
):
    order = Order()
    pipe, dp, tensor = order.pipe, order.dp, order.tensor
    n_pipe, n_dp, n_tensor = order.n_pipe, order.n_dp, order.n_tensor
    first = pipe == 0

    stream = ends[0]
    all_count, quarter, width = stream.shape
    count = all_count // n_pipe
    rows = count * quarter
    length = segments.shape[1]
    channels = mix_in.shape[3]
    hidden = gate_up.shape[3]
    head_size = qk_gains.shape[1]
    full = channels * n_tensor
    heads = full // head_size
    kv_heads = heads // 2
    group = heads // kv_heads
    scale = 1.0 / head_size**0.5

    mix_raw = jnp.concatenate([mix_in[0, :, 0], mix_in[0, :, 1], mix_out[0].T], axis=1)
    kept = jnp.where(first, stream[:count], stream[count:])
    given = jnp.where(first, stream[count:], stream[:count])
    came = by_xor(given, PIPE, 1)
    h0 = order.to_local(jnp.where(first, kept, came).reshape(rows, width))
    cot = order.to_local(jnp.where(first, came, kept).reshape(rows, width))
    g_one = order.to_local(gains_one)
    g_two = order.to_local(gains_two)
    seg = jnp.where(first, segments[:count], segments[count:])

    def halves(raw):
        size = raw.shape[0] // 2
        low, high = raw[:size], raw[size:]
        mine = jnp.where(first, low, high)
        recv = by_xor(jnp.where(first, high, low), PIPE, 1)
        return (jnp.where(first, mine, recv), jnp.where(first, recv, mine))

    mix_one, mix_two = halves(mix_raw)
    value_pairs = []
    for a in range(n_pipe):
        for b in range(n_dp):
            k = b * n_pipe + a
            value_pairs.append((k, a * n_dp + b))
    value_half = lax.ppermute(value_weight, (PIPE, DP), value_pairs)
    out_one = jnp.concatenate(z_gather(mix_one[:, 2 * channels :]), axis=1)
    in_half = jnp.concatenate([mix_one[:, : 2 * channels], value_half], axis=1)
    w_bcx = xor_gather(in_half, dp)
    w_out1 = dp_gather(out_one)

    def whole_width(mine, other):
        return jnp.concatenate(
            [jnp.where(first, mine, other), jnp.where(first, other, mine)], axis=-1
        )

    ffn_raw = jnp.concatenate([gate_up[0, :, 0], gate_up[0, :, 1], down[0].T], axis=1)
    ffn_one, ffn_two = halves(ffn_raw)
    w_ffn1 = dp_gather(ffn_one)
    parts_two = z_gather(mix_two)
    parts_two = xor_list(parts_two, tensor)
    pack_two = jnp.concatenate(
        [piece[:, i * channels : (i + 1) * channels] for i in range(3) for piece in parts_two],
        axis=1,
    )
    w_two = dp_gather(pack_two)
    w_ffn2 = dp_gather(ffn_two)
    w_qkv, w_out2 = w_two[:, : 2 * full], w_two[:, 2 * full :]

    a1, n1, r1 = norm_forward(h0, g_one[0])
    a1_list = z_gather(a1.astype(BF).reshape(count, quarter, width))
    a1_rows = jnp.concatenate(xor_list(a1_list, tensor), axis=1).reshape(count * length, width)
    kernel = lax.dynamic_slice_in_dim(conv_kernel, tensor * channels, channels, 1)
    a1_halves = by_half(a1_rows, first)
    bcx = dot(a1_halves[0], w_bcx[0]) + dot(a1_halves[1], w_bcx[1])
    bcx = bcx.reshape(count, length, 3 * channels)
    bgate, cgate, values = cut(bcx, 3)
    mixed = bgate * values
    convolved = kernel[2] * mixed + kernel[1] * delay(mixed, 1) + kernel[0] * delay(mixed, 2)
    gated = (cgate * convolved).astype(BF)
    y_list = xor_list(cut(gated, n_tensor, 1), tensor)
    y_list = [y_list[0]] + [by_xor(y_list[s], TENSOR, s) for s in others(TENSOR)]
    y_full = jnp.concatenate(y_list, axis=-1).reshape(rows, full)
    h1 = h0 + dot_nt(y_full, w_out1)

    def ffn_parts(w):
        return (w[:, :hidden], w[:, hidden : 2 * hidden], w[:, 2 * hidden :])

    a2, n2, r2 = norm_forward(h1, g_one[1])
    a2_rows = jnp.concatenate(z_gather(a2.astype(BF)), axis=0)
    cot_rows = jnp.concatenate(z_gather(cot.astype(BF)), axis=0)
    wg1, wu1, wd1 = ffn_parts(w_ffn1)
    gate1 = dot(a2_rows, wg1)
    up1 = dot(a2_rows, wu1)
    z1 = (jax.nn.silu(gate1) * up1).astype(BF)
    out1 = h1 + z_scatter(cut(dot_nt(z1, wd1), n_tensor, 0))

    a3, n3, r3 = norm_forward(out1, g_two[0])
    a3_half = a3.astype(BF)
    qkv = dot(a3_half, w_qkv)
    query = qkv[:, :full].reshape(count, quarter, heads, head_size)
    paired = qkv[:, full:].reshape(count, quarter, kv_heads, 2, head_size)
    q_out, q_norm, q_recip = norm_forward(query, qk_gains[0])
    k_out, k_norm, k_recip = norm_forward(paired[:, :, :, 0], qk_gains[1])
    start = tensor * quarter
    seg_own = lax.dynamic_slice_in_dim(seg, start, quarter, 1)
    before = jnp.sum((seg[:, None, :] < seg_own[:, :, None]).astype(jnp.int32), axis=-1)
    index = start + lax.broadcasted_iota(jnp.int32, (count, quarter), 1)
    position = (index - before).astype(F32)
    freqs = THETA ** (-2.0 * jnp.arange(head_size // 2, dtype=F32) / head_size)
    angle = position[:, :, None] * freqs
    cosine, sine = jnp.cos(angle)[:, :, None, :], jnp.sin(angle)[:, :, None, :]
    q_half = rotate(q_out, cosine, sine).astype(BF).reshape(
        count, quarter, kv_heads, group, head_size
    )
    k_half = rotate(k_out, cosine, sine).astype(BF)
    v_half = paired[:, :, :, 1].astype(BF)
    reach = min(-(-(LONGEST - 1) // quarter), n_tensor - 1)
    kv_own = jnp.stack([k_half, v_half])
    kv_parts = [kv_own]
    for _ in range(1, reach + 1):
        kv_parts.insert(0, by_shift(kv_parts[0], TENSOR, 1))
    kv = jnp.concatenate(kv_parts, axis=2)
    keys, vals = kv[0], kv[1]
    span = (reach + 1) * quarter
    seg_keys = lax.dynamic_slice_in_dim(
        jnp.pad(seg, ((0, 0), (reach * quarter, 0)), constant_values=-1), start, span, 1
    )
    row_at = lax.broadcasted_iota(jnp.int32, (quarter, span), 0) + reach * quarter
    col_at = lax.broadcasted_iota(jnp.int32, (quarter, span), 1)
    allowed = (seg_own[:, :, None] == seg_keys[:, None, :]) & (col_at <= row_at)[None]
    scores = (
        jnp.einsum("sangd,sbnd->sngab", q_half, keys, preferred_element_type=F32) * scale
    )
    masked = jnp.where(allowed[:, None, None], scores, NEG)
    highest = jnp.max(masked, axis=-1, keepdims=True)
    lse = highest + jnp.log(jnp.sum(jnp.exp(masked - highest), axis=-1, keepdims=True))
    prob = jnp.exp(masked - lse)
    p_half = prob.astype(BF)
    attended = jnp.einsum("sngab,sbnd->sangd", p_half, vals, preferred_element_type=F32)
    o_local = attended.astype(BF).reshape(rows, full)
    h3 = out1 + dot_nt(o_local, w_out2)

    a4, n4, r4 = norm_forward(h3, g_two[1])
    a4_rows = jnp.concatenate(z_gather(a4.astype(BF)), axis=0)

    def ffn_backward(a_rows, gate, up, zed, c_rows, w):
        wg, wu, wd = ffn_parts(w)
        grad_hidden = dot(c_rows, wd)
        sigma = jax.nn.sigmoid(gate)
        grad_gate = (grad_hidden * up * sigma * (1.0 + gate * (1.0 - sigma))).astype(BF)
        grad_up = (grad_hidden * gate * sigma).astype(BF)
        back = dot_nt(grad_gate, wg) + dot_nt(grad_up, wu)
        back = z_scatter(cut(back, n_tensor, 0))
        total = pair_grad((a_rows, a_rows, c_rows), (grad_gate, grad_up, zed), first)
        return (back, dp_scatter(total))

    wg2, wu2, wd2 = ffn_parts(w_ffn2)
    gate2 = dot(a4_rows, wg2)
    up2 = dot(a4_rows, wu2)
    z2 = (jax.nn.silu(gate2) * up2).astype(BF)
    da4, r_ffn2 = ffn_backward(a4_rows, gate2, up2, z2, cot_rows, w_ffn2)
    o2_part = dot_nt(z2, wd2)
    o2_parts = [part.astype(BF) for part in cut(o2_part, n_tensor, 0)]
    o2_parts = [o2_parts[0]] + [by_xor(o2_parts[s], TENSOR, s) for s in others(TENSOR)]
    out2 = add_all(h3, o2_parts, n_pipe, n_dp).reshape(count, quarter, width)
    back4, d_gain4 = norm_backward(da4, n4, r4, g_two[1])
    dh3 = cot + back4

    db3 = dh3.astype(BF)
    do_half = dot(db3, w_out2).astype(BF)
    do_half = do_half.reshape(count, quarter, kv_heads, group, head_size)
    grad_prob = jnp.einsum("sangd,sbnd->sngab", do_half, vals, preferred_element_type=F32)
    delta = jnp.sum(prob * grad_prob, axis=-1, keepdims=True)
    ds = (prob * (grad_prob - delta)).astype(BF)
    dv = jnp.einsum("sngab,sangd->sbnd", p_half, do_half, preferred_element_type=F32)
    dq = jnp.einsum("sngab,sbnd->sangd", ds, keys, preferred_element_type=F32) * scale
    dk = jnp.einsum("sngab,sangd->sbnd", ds, q_half, preferred_element_type=F32) * scale
    dkv = jnp.stack([dk, dv])
    total = dkv[:, :, reach * quarter :]
    came = None
    for j in range(reach, 0, -1):
        part = dkv[:, :, (reach - j) * quarter : (reach - j + 1) * quarter]
        if came is not None:
            part = part + came.astype(F32)
        came = by_shift(part.astype(BF), TENSOR, -1)
    if came is not None:
        total = total + came.astype(F32)
    dq = rotate_back(dq.reshape(count, quarter, heads, head_size), cosine, sine)
    dk = rotate_back(total[0], cosine, sine)
    dq, d_qgain = norm_backward(dq, q_norm, q_recip, qk_gains[0])
    dk, d_kgain = norm_backward(dk, k_norm, k_recip, qk_gains[1])
    dq = dq.astype(BF).reshape(rows, full)
    dkv = jnp.stack([dk, total[1]], axis=3).astype(BF).reshape(rows, full)
    dqkv = jnp.concatenate([dq, dkv], axis=1)
    d_two = pair_grad((a3_half, db3), (dqkv, o_local), first)
    r_two = xor_scatter(d_two, dp)
    back3, d_gain3 = norm_backward(dot_nt(dqkv, w_qkv), n3, r3, g_two[0])
    dout1 = dh3 + back3

    c1_rows = jnp.concatenate(z_gather(dout1.astype(BF)), axis=0)
    da2, r_ffn1 = ffn_backward(a2_rows, gate1, up1, z1, c1_rows, w_ffn1)
    back2, d_gain2 = norm_backward(da2, n2, r2, g_one[1])
    dh1 = dout1 + back2

    db1 = dh1.astype(BF)
    dy = dot(db1, w_out1)
    dy_list = cut(dy.astype(BF).reshape(count, quarter, full), n_tensor)
    dy_list = [dy_list[0]] + [by_xor(dy_list[s], TENSOR, s) for s in others(TENSOR)]
    dy = jnp.concatenate(xor_list(dy_list, tensor), axis=1).astype(F32)
    d_out1 = pair_grad((db1,), (y_full,), first)
    du = dy * cgate
    dc = (dy * convolved).astype(BF)
    dm = kernel[2] * du + kernel[1] * advance(du, 1) + kernel[0] * advance(du, 2)
    d_kernel = jnp.stack(
        [
            jnp.sum(du * delay(mixed, 2), axis=(0, 1)),
            jnp.sum(du * delay(mixed, 1), axis=(0, 1)),
            jnp.sum(du * mixed, axis=(0, 1)),
        ]
    )
    dbcx = jnp.concatenate([(dm * values).astype(BF), dc, (dm * bgate).astype(BF)], axis=-1)
    dbcx_rows = dbcx.reshape(count * length, 3 * channels)
    d_bcx = pair_grad((a1_halves,), (dbcx_rows,), first)
    da1 = whole_width(dot_nt(dbcx_rows, w_bcx[0]), dot_nt(dbcx_rows, w_bcx[1]))
    d_gain1 = jnp.sum(da1 * a1_rows.astype(F32), axis=0) / g_one[0]
    da1 = da1.reshape(count, length, width)
    da1 = z_scatter(xor_list(cut(da1, n_tensor, 1), tensor)).reshape(rows, width)
    back1, _ = norm_backward(da1, n1, r1, g_one[0])
    dh0 = dh1 + back1

    blocks = cut(r_two.astype(BF), 3 * n_tensor)
    r_two = jnp.concatenate(
        [jnp.concatenate(blocks[z::n_tensor], axis=1) for z in range(n_tensor)], axis=0
    )
    r_two = lax.psum_scatter(r_two, TENSOR, scatter_dimension=0, tiled=True).astype(F32)
    r_out1 = z_scatter(cut(xor_scatter(d_out1, dp), n_tensor))
    r_bcx = xor_scatter(d_bcx, dp)
    r_bc, r_x = r_bcx[:, : 2 * channels], r_bcx[:, 2 * channels :]

    def whole(one, one_came, two, two_came):
        mine = jnp.where(first, one, two)
        came = jnp.where(first, one_came, two_came)
        return jnp.concatenate(
            [jnp.where(first, mine, came), jnp.where(first, came, mine)], axis=0
        )

    def sent_to(owner, value):
        return lax.ppermute(value.astype(BF), PIPE, [(1 - owner, owner)]).astype(F32)

    ffn2_came = sent_to(1, r_ffn2)
    ffn1_came = sent_to(0, r_ffn1)
    g_ffn = whole(r_ffn1, ffn1_came, r_ffn2, ffn2_came)
    gate_up_grad = jnp.stack([g_ffn[:, :hidden], g_ffn[:, hidden : 2 * hidden]], axis=1)
    down_grad = g_ffn[:, 2 * hidden :].T
    mix2_came = sent_to(1, r_two)
    r_mix1 = jnp.concatenate([r_bc, r_out1], axis=1)
    mix1_came = sent_to(0, r_mix1)
    g_mix = whole(r_mix1, mix1_came, r_two, mix2_came)
    mix_in_grad = jnp.stack([g_mix[:, :channels], g_mix[:, channels : 2 * channels]], axis=1)
    mix_out_grad = g_mix[:, 2 * channels :].T
    value_grad = lax.ppermute(r_x, (PIPE, DP), [(b, a) for a, b in value_pairs])

    kernel_full = lax.dynamic_update_slice_in_dim(
        jnp.zeros(conv_kernel.shape, F32), d_kernel, tensor * channels, 1
    )
    gain_rows = order.to_true(jnp.stack([d_gain1, d_gain2, d_gain3, d_gain4]))
    qk_row = jnp.concatenate([d_qgain, d_kgain])[None]
    qk_row = jnp.pad(qk_row, ((0, 0), (0, width - qk_row.shape[1])))
    sums = all_sum(jnp.concatenate([gain_rows, kernel_full, qk_row], axis=0))
    taps = conv_kernel.shape[0]
    sum_kernel = sums[4 : 4 + taps]
    sum_qk = sums[4 + taps, : 2 * head_size].reshape(2, head_size)

    dh0 = order.to_true(dh0).reshape(count, quarter, width)
    recv = by_xor(jnp.where(first, out2, dh0), PIPE, 1)
    ends_out = jnp.concatenate(
        [jnp.where(first, dh0, recv), jnp.where(first, recv, out2)], axis=0
    )
    return (
        ends_out[None],
        mix_in_grad[None],
        mix_out_grad[None],
        gate_up_grad[None],
        down_grad[None],
        value_grad,
        sums[0:2],
        sums[2:4],
        sum_kernel,
        sum_qk,
    )


def solution(mesh):
    return jax.shard_map(
        compute,
        mesh=mesh,
        in_specs=(
            P(PIPE, DP, TENSOR, None),
            P(PIPE, DP, None, TENSOR),
            P(PIPE, TENSOR, DP),
            P(PIPE, DP, None, TENSOR),
            P(PIPE, TENSOR, DP),
            P((PIPE, DP), TENSOR),
            P(),
            P(),
            P(),
            P(),
            P(DP, None),
        ),
        out_specs=(
            P(PIPE, DP, TENSOR, None),
            P(PIPE, DP, None, TENSOR),
            P(PIPE, TENSOR, DP),
            P(PIPE, DP, None, TENSOR),
            P(PIPE, TENSOR, DP),
            P((PIPE, DP), TENSOR),
            P(),
            P(),
            P(),
            P(),
        ),
        check_vma=False,
    )
```

```python
import jax
import jax.numpy as jnp
from jax import lax
from jax.experimental import pallas as pl
from jax.experimental.pallas import tpu as pltpu
from jax.sharding import PartitionSpec as P


EPS = 1e-05
THETA = 1000000.0
NEG = -1e30
LONGEST = 256


PIPE, DP, TENSOR = "pipe", "dp", "tensor"
BF = jnp.bfloat16
F32 = jnp.float32


def dot(a, b):
    return jnp.dot(a, b, preferred_element_type=F32)


def dot_tn(a, b):
    return lax.dot_general(a, b, (((0,), (0,)), ((), ())), preferred_element_type=F32)


def dot_nt(a, b):
    return lax.dot_general(a, b, (((1,), (1,)), ((), ())), preferred_element_type=F32)


def by_xor(value, axis, mask):
    size = lax.axis_size(axis)
    return lax.ppermute(value, axis, [(i, i ^ mask) for i in range(size)])


def by_shift(value, axis, by):
    size = lax.axis_size(axis)
    pairs = [(i, i + by) for i in range(size) if 0 <= i + by < size]
    return lax.ppermute(value, axis, pairs)


def others(axis):
    return range(1, lax.axis_size(axis))


def xor_list(items, index):
    bit = 1
    while bit < len(items):
        on = (index & bit) != 0
        items = [jnp.where(on, items[i ^ bit], items[i]) for i in range(len(items))]
        bit *= 2
    return items


def cut(value, count, axis=-1):
    return jnp.split(value, count, axis=axis)


class Order:
    def __init__(self):
        self.pipe = lax.axis_index(PIPE)
        self.dp = lax.axis_index(DP)
        self.tensor = lax.axis_index(TENSOR)
        self.n_pipe = lax.axis_size(PIPE)
        self.n_dp = lax.axis_size(DP)
        self.n_tensor = lax.axis_size(TENSOR)

    def to_local(self, value):
        pieces = cut(value, self.n_dp * self.n_pipe)
        moved = [pieces[c * self.n_pipe + q] for q in range(self.n_pipe) for c in range(self.n_dp)]
        return jnp.concatenate(moved, axis=-1)

    def to_true(self, value):
        pieces = cut(value, self.n_dp * self.n_pipe)
        moved = [pieces[q * self.n_dp + c] for c in range(self.n_dp) for q in range(self.n_pipe)]
        return jnp.concatenate(moved, axis=-1)


def norm_forward(values, gain):
    recip = lax.rsqrt(jnp.mean(values * values, axis=-1, keepdims=True) + EPS)
    normed = values * recip
    return (normed * gain, normed, recip)


def norm_backward(grad, normed, recip, gain):
    scaled = grad * gain
    back = recip * (scaled - normed * jnp.mean(scaled * normed, axis=-1, keepdims=True))
    return (back, jnp.sum(grad * normed, axis=tuple(range(grad.ndim - 1))))


def add_all(stream, pieces, n_pipe, n_dp):
    rows, width = stream.shape
    size = width // (n_pipe * n_dp)

    def body(*refs):
        for q in range(n_pipe):
            for c in range(n_dp):
                local = pl.ds((q * n_dp + c) * size, size)
                total = refs[0][:, local]
                for ref in refs[1:-1]:
                    total = total + ref[:, local].astype(F32)
                refs[-1][:, pl.ds((c * n_pipe + q) * size, size)] = total

    return pl.pallas_call(body, out_shape=jax.ShapeDtypeStruct((rows, width), F32))(
        stream, *pieces
    )


def assemble(pieces, index):
    count = len(pieces)
    height, width = pieces[0].shape

    def body(index_ref, *refs):
        for i in range(count):
            at = jnp.bitwise_xor(index_ref[0], i) * height
            refs[-1][pl.ds(pl.multiple_of(at, height), height), :] = refs[i][...]

    whole = pl.BlockSpec(memory_space=pltpu.MemorySpace.VMEM)
    return pl.pallas_call(
        body,
        out_shape=jax.ShapeDtypeStruct((count * height, width), pieces[0].dtype),
        in_specs=[pl.BlockSpec(memory_space=pltpu.MemorySpace.SMEM)] + [whole] * count,
        out_specs=whole,
    )(index.reshape(1).astype(jnp.int32), *pieces)


def xor_gather(half, dp):
    pieces = [half] + [by_xor(half, DP, s) for s in others(DP)]
    mine = assemble(pieces, dp)
    return (mine, by_xor(mine, PIPE, 1))


def z_gather(rows):
    return [rows] + [by_xor(rows, TENSOR, s) for s in others(TENSOR)]


def z_scatter(parts):
    moved = [by_xor(parts[s].astype(BF), TENSOR, s) for s in others(TENSOR)]
    total = parts[0].astype(F32)
    for piece in moved:
        total = total + piece.astype(F32)
    return total


def dp_gather(half):
    return lax.all_gather(half, (PIPE, DP), axis=0, tiled=True)


def by_half(value, first):
    low, high = cut(value, 2)
    return (jnp.where(first, low, high), jnp.where(first, high, low))


def pair_grad(lefts, rights, first):
    halves = [left if isinstance(left, tuple) else by_half(left, first) for left in lefts]
    sent = []
    for (_, left), right in zip(halves, rights, strict=True):
        sent.append(dot_tn(left, right).astype(BF))
    came = [by_xor(piece, PIPE, 1) for piece in sent]
    sums = [
        (dot_tn(left, right) + piece.astype(F32)).astype(BF)
        for (left, _), right, piece in zip(halves, rights, came, strict=True)
    ]
    return sums[0] if len(sums) == 1 else jnp.concatenate(sums, axis=1)


def dp_scatter(total):
    return lax.psum_scatter(total, DP, scatter_dimension=0, tiled=True).astype(F32)


def tree_sum(parts):
    parts = [part.astype(F32) for part in parts]
    while len(parts) > 1:
        parts = [parts[i] + parts[i + 1] for i in range(0, len(parts), 2)]
    return parts[0]


def xor_scatter(total, dp, shared=None):
    size = total.shape[0] // lax.axis_size(DP)
    pieces = [
        lax.dynamic_slice_in_dim(total, (dp ^ s) * size, size, 0)
        for s in range(lax.axis_size(DP))
    ]
    if shared is not None:
        pieces = [jnp.concatenate([piece, shared], axis=1) for piece in pieces]
    moved = [by_xor(pieces[s], DP, s) for s in others(DP)]
    return tree_sum([pieces[0]] + moved)


def delay(values, steps):
    return jnp.pad(values, ((0, 0), (steps, 0), (0, 0)))[:, : values.shape[1]]


def advance(values, steps):
    return jnp.pad(values, ((0, 0), (0, steps), (0, 0)))[:, steps:]


def rotate(values, cosine, sine):
    half = values.shape[-1] // 2
    first, second = (values[..., :half], values[..., half:])
    return jnp.concatenate(
        [first * cosine - second * sine, second * cosine + first * sine], axis=-1
    )


def rotate_back(grad, cosine, sine):
    half = grad.shape[-1] // 2
    first, second = (grad[..., :half], grad[..., half:])
    return jnp.concatenate(
        [first * cosine + second * sine, second * cosine - first * sine], axis=-1
    )


def compute(
    ends,
    mix_in,
    mix_out,
    gate_up,
    down,
    value_weight,
    gains_one,
    gains_two,
    conv_kernel,
    qk_gains,
    segments,
):
    order = Order()
    pipe, dp, tensor = order.pipe, order.dp, order.tensor
    n_pipe, n_dp, n_tensor = order.n_pipe, order.n_dp, order.n_tensor
    first = pipe == 0

    stream = ends[0]
    all_count, quarter, width = stream.shape
    count = all_count // n_pipe
    rows = count * quarter
    length = segments.shape[1]
    channels = mix_in.shape[3]
    hidden = gate_up.shape[3]
    head_size = qk_gains.shape[1]
    full = channels * n_tensor
    heads = full // head_size
    kv_heads = heads // 2
    group = heads // kv_heads
    scale = 1.0 / head_size**0.5

    mix_raw = jnp.concatenate([mix_in[0, :, 0], mix_in[0, :, 1], mix_out[0].T], axis=1)
    kept = jnp.where(first, stream[:count], stream[count:])
    given = jnp.where(first, stream[count:], stream[:count])
    came = by_xor(given, PIPE, 1)
    h0 = order.to_local(jnp.where(first, kept, came).reshape(rows, width))
    cot = order.to_local(jnp.where(first, came, kept).reshape(rows, width))
    g_one = order.to_local(gains_one)
    g_two = order.to_local(gains_two)
    seg = jnp.where(first, segments[:count], segments[count:])

    def halves(raw):
        size = raw.shape[0] // 2
        low, high = raw[:size], raw[size:]
        mine = jnp.where(first, low, high)
        recv = by_xor(jnp.where(first, high, low), PIPE, 1)
        return (jnp.where(first, mine, recv), jnp.where(first, recv, mine))

    mix_one, mix_two = halves(mix_raw)
    value_pairs = []
    for a in range(n_pipe):
        for b in range(n_dp):
            k = b * n_pipe + a
            value_pairs.append((k, a * n_dp + b))
    value_half = lax.ppermute(value_weight, (PIPE, DP), value_pairs)
    out_one = jnp.concatenate(z_gather(mix_one[:, 2 * channels :]), axis=1)
    in_half = jnp.concatenate([mix_one[:, : 2 * channels], value_half], axis=1)
    w_bcx = xor_gather(in_half, dp)
    w_out1 = dp_gather(out_one)

    def whole_width(mine, other):
        return jnp.concatenate(
            [jnp.where(first, mine, other), jnp.where(first, other, mine)], axis=-1
        )

    ffn_raw = jnp.concatenate([gate_up[0, :, 0], gate_up[0, :, 1], down[0].T], axis=1)
    ffn_one, ffn_two = halves(ffn_raw)
    w_ffn1 = dp_gather(ffn_one)
    parts_two = z_gather(mix_two)
    parts_two = xor_list(parts_two, tensor)
    pack_two = jnp.concatenate(
        [piece[:, i * channels : (i + 1) * channels] for i in range(3) for piece in parts_two],
        axis=1,
    )
    w_two = dp_gather(pack_two)
    w_ffn2 = dp_gather(ffn_two)
    w_qkv, w_out2 = w_two[:, : 2 * full], w_two[:, 2 * full :]

    a1, n1, r1 = norm_forward(h0, g_one[0])
    a1_list = z_gather(a1.astype(BF).reshape(count, quarter, width))
    a1_rows = jnp.concatenate(xor_list(a1_list, tensor), axis=1).reshape(count * length, width)
    kernel = lax.dynamic_slice_in_dim(conv_kernel, tensor * channels, channels, 1)
    a1_halves = by_half(a1_rows, first)
    bcx = dot(a1_halves[0], w_bcx[0]) + dot(a1_halves[1], w_bcx[1])
    bcx = bcx.reshape(count, length, 3 * channels)
    bgate, cgate, values = cut(bcx, 3)
    mixed = bgate * values
    convolved = kernel[2] * mixed + kernel[1] * delay(mixed, 1) + kernel[0] * delay(mixed, 2)
    gated = (cgate * convolved).astype(BF)
    y_list = xor_list(cut(gated, n_tensor, 1), tensor)
    y_list = [y_list[0]] + [by_xor(y_list[s], TENSOR, s) for s in others(TENSOR)]
    y_full = jnp.concatenate(y_list, axis=-1).reshape(rows, full)
    h1 = h0 + dot_nt(y_full, w_out1)

    def ffn_parts(w):
        return (w[:, :hidden], w[:, hidden : 2 * hidden], w[:, 2 * hidden :])

    a2, n2, r2 = norm_forward(h1, g_one[1])
    a2_rows = jnp.concatenate(z_gather(a2.astype(BF)), axis=0)
    cot_rows = jnp.concatenate(z_gather(cot.astype(BF)), axis=0)
    wg1, wu1, wd1 = ffn_parts(w_ffn1)
    gate1 = dot(a2_rows, wg1)
    up1 = dot(a2_rows, wu1)
    z1 = (jax.nn.silu(gate1) * up1).astype(BF)
    out1 = h1 + z_scatter(cut(dot_nt(z1, wd1), n_tensor, 0))

    a3, n3, r3 = norm_forward(out1, g_two[0])
    a3_half = a3.astype(BF)
    qkv = dot(a3_half, w_qkv)
    query = qkv[:, :full].reshape(count, quarter, heads, head_size)
    paired = qkv[:, full:].reshape(count, quarter, kv_heads, 2, head_size)
    q_out, q_norm, q_recip = norm_forward(query, qk_gains[0])
    k_out, k_norm, k_recip = norm_forward(paired[:, :, :, 0], qk_gains[1])
    start = tensor * quarter
    seg_own = lax.dynamic_slice_in_dim(seg, start, quarter, 1)
    before = jnp.sum((seg[:, None, :] < seg_own[:, :, None]).astype(jnp.int32), axis=-1)
    index = start + lax.broadcasted_iota(jnp.int32, (count, quarter), 1)
    position = (index - before).astype(F32)
    freqs = THETA ** (-2.0 * jnp.arange(head_size // 2, dtype=F32) / head_size)
    angle = position[:, :, None] * freqs
    cosine, sine = jnp.cos(angle)[:, :, None, :], jnp.sin(angle)[:, :, None, :]
    q_half = rotate(q_out, cosine, sine).astype(BF).reshape(
        count, quarter, kv_heads, group, head_size
    )
    k_half = rotate(k_out, cosine, sine).astype(BF)
    v_half = paired[:, :, :, 1].astype(BF)
    reach = min(-(-(LONGEST - 1) // quarter), n_tensor - 1)
    kv_own = jnp.stack([k_half, v_half])
    kv_parts = [kv_own]
    for _ in range(1, reach + 1):
        kv_parts.insert(0, by_shift(kv_parts[0], TENSOR, 1))
    kv = jnp.concatenate(kv_parts, axis=2)
    keys, vals = kv[0], kv[1]
    span = (reach + 1) * quarter
    seg_keys = lax.dynamic_slice_in_dim(
        jnp.pad(seg, ((0, 0), (reach * quarter, 0)), constant_values=-1), start, span, 1
    )
    row_at = lax.broadcasted_iota(jnp.int32, (quarter, span), 0) + reach * quarter
    col_at = lax.broadcasted_iota(jnp.int32, (quarter, span), 1)
    allowed = (seg_own[:, :, None] == seg_keys[:, None, :]) & (col_at <= row_at)[None]
    scores = (
        jnp.einsum("sangd,sbnd->sngab", q_half, keys, preferred_element_type=F32) * scale
    )
    masked = jnp.where(allowed[:, None, None], scores, NEG)
    highest = jnp.max(masked, axis=-1, keepdims=True)
    lse = highest + jnp.log(jnp.sum(jnp.exp(masked - highest), axis=-1, keepdims=True))
    prob = jnp.exp(masked - lse)
    p_half = prob.astype(BF)
    attended = jnp.einsum("sngab,sbnd->sangd", p_half, vals, preferred_element_type=F32)
    o_local = attended.astype(BF).reshape(rows, full)
    h3 = out1 + dot_nt(o_local, w_out2)

    a4, n4, r4 = norm_forward(h3, g_two[1])
    a4_rows = jnp.concatenate(z_gather(a4.astype(BF)), axis=0)

    def ffn_backward(a_rows, gate, up, zed, c_rows, w):
        wg, wu, wd = ffn_parts(w)
        grad_hidden = dot(c_rows, wd)
        sigma = jax.nn.sigmoid(gate)
        grad_gate = (grad_hidden * up * sigma * (1.0 + gate * (1.0 - sigma))).astype(BF)
        grad_up = (grad_hidden * gate * sigma).astype(BF)
        back = dot_nt(grad_gate, wg) + dot_nt(grad_up, wu)
        back = z_scatter(cut(back, n_tensor, 0))
        total = pair_grad((a_rows, a_rows, c_rows), (grad_gate, grad_up, zed), first)
        return (back, dp_scatter(total))

    wg2, wu2, wd2 = ffn_parts(w_ffn2)
    gate2 = dot(a4_rows, wg2)
    up2 = dot(a4_rows, wu2)
    z2 = (jax.nn.silu(gate2) * up2).astype(BF)
    da4, r_ffn2 = ffn_backward(a4_rows, gate2, up2, z2, cot_rows, w_ffn2)
    o2_part = dot_nt(z2, wd2)
    o2_parts = [part.astype(BF) for part in cut(o2_part, n_tensor, 0)]
    o2_parts = [o2_parts[0]] + [by_xor(o2_parts[s], TENSOR, s) for s in others(TENSOR)]
    out2 = add_all(h3, o2_parts, n_pipe, n_dp).reshape(count, quarter, width)
    back4, d_gain4 = norm_backward(da4, n4, r4, g_two[1])
    dh3 = cot + back4

    db3 = dh3.astype(BF)
    do_half = dot(db3, w_out2).astype(BF)
    do_half = do_half.reshape(count, quarter, kv_heads, group, head_size)
    grad_prob = jnp.einsum("sangd,sbnd->sngab", do_half, vals, preferred_element_type=F32)
    delta = jnp.sum(prob * grad_prob, axis=-1, keepdims=True)
    ds = (prob * (grad_prob - delta)).astype(BF)
    dv = jnp.einsum("sngab,sangd->sbnd", p_half, do_half, preferred_element_type=F32)
    dq = jnp.einsum("sngab,sbnd->sangd", ds, keys, preferred_element_type=F32) * scale
    dk = jnp.einsum("sngab,sangd->sbnd", ds, q_half, preferred_element_type=F32) * scale
    dkv = jnp.stack([dk, dv])
    total = dkv[:, :, reach * quarter :]
    came = None
    for j in range(reach, 0, -1):
        part = dkv[:, :, (reach - j) * quarter : (reach - j + 1) * quarter]
        if came is not None:
            part = part + came.astype(F32)
        came = by_shift(part.astype(BF), TENSOR, -1)
    if came is not None:
        total = total + came.astype(F32)
    dq = rotate_back(dq.reshape(count, quarter, heads, head_size), cosine, sine)
    dk = rotate_back(total[0], cosine, sine)
    dq, d_qgain = norm_backward(dq, q_norm, q_recip, qk_gains[0])
    dk, d_kgain = norm_backward(dk, k_norm, k_recip, qk_gains[1])
    dq = dq.astype(BF).reshape(rows, full)
    dkv = jnp.stack([dk, total[1]], axis=3).astype(BF).reshape(rows, full)
    dqkv = jnp.concatenate([dq, dkv], axis=1)
    d_two = pair_grad((a3_half, db3), (dqkv, o_local), first)
    r_two = xor_scatter(d_two, dp)
    back3, d_gain3 = norm_backward(dot_nt(dqkv, w_qkv), n3, r3, g_two[0])
    dout1 = dh3 + back3

    c1_rows = jnp.concatenate(z_gather(dout1.astype(BF)), axis=0)
    da2, r_ffn1 = ffn_backward(a2_rows, gate1, up1, z1, c1_rows, w_ffn1)
    back2, d_gain2 = norm_backward(da2, n2, r2, g_one[1])
    dh1 = dout1 + back2

    db1 = dh1.astype(BF)
    dy = dot(db1, w_out1)
    dy_list = cut(dy.astype(BF).reshape(count, quarter, full), n_tensor)
    dy_list = [dy_list[0]] + [by_xor(dy_list[s], TENSOR, s) for s in others(TENSOR)]
    dy = jnp.concatenate(xor_list(dy_list, tensor), axis=1).astype(F32)
    d_out1 = pair_grad((db1,), (y_full,), first)
    du = dy * cgate
    dc = (dy * convolved).astype(BF)
    dm = kernel[2] * du + kernel[1] * advance(du, 1) + kernel[0] * advance(du, 2)
    d_kernel = jnp.stack(
        [
            jnp.sum(du * delay(mixed, 2), axis=(0, 1)),
            jnp.sum(du * delay(mixed, 1), axis=(0, 1)),
            jnp.sum(du * mixed, axis=(0, 1)),
        ]
    )
    dbcx = jnp.concatenate([(dm * values).astype(BF), dc, (dm * bgate).astype(BF)], axis=-1)
    dbcx_rows = dbcx.reshape(count * length, 3 * channels)
    d_bcx = pair_grad((a1_halves,), (dbcx_rows,), first)
    da1 = whole_width(dot_nt(dbcx_rows, w_bcx[0]), dot_nt(dbcx_rows, w_bcx[1]))
    d_gain1 = jnp.sum(da1 * a1_rows.astype(F32), axis=0) / g_one[0]
    da1 = da1.reshape(count, length, width)
    da1 = z_scatter(xor_list(cut(da1, n_tensor, 1), tensor)).reshape(rows, width)
    back1, _ = norm_backward(da1, n1, r1, g_one[0])
    dh0 = dh1 + back1

    piece_rows = d_bcx.shape[0] // n_dp
    blocks = cut(r_two.astype(BF), 3 * n_tensor)
    r_two = jnp.concatenate(
        [jnp.concatenate(blocks[z::n_tensor], axis=1) for z in range(n_tensor)], axis=0
    )
    parts = [
        lax.dynamic_slice_in_dim(r_two, (tensor ^ z) * piece_rows, piece_rows, 0)
        for z in range(n_tensor)
    ]
    r_two = z_scatter(parts)
    kernel_full = lax.dynamic_update_slice_in_dim(
        jnp.zeros(conv_kernel.shape, F32), d_kernel, tensor * channels, 1
    )
    gain_rows = order.to_true(jnp.stack([d_gain1, d_gain2, d_gain3, d_gain4]))
    qk_row = jnp.concatenate([d_qgain, d_kgain])[None]
    qk_row = jnp.pad(qk_row, ((0, 0), (0, width - qk_row.shape[1])))
    sums = jnp.concatenate([gain_rows, kernel_full, qk_row], axis=0)
    n_sums = sums.shape[0]
    sums = sums + by_xor(sums, PIPE, 1)
    shared = sums.astype(BF).reshape(piece_rows, n_sums * width // piece_rows)
    r_out1 = xor_scatter(d_out1, dp)
    r_bcx = xor_scatter(d_bcx, dp, shared)
    r_bc, r_x = r_bcx[:, : 2 * channels], r_bcx[:, 2 * channels : 3 * channels]
    shared = r_bcx[:, 3 * channels :].astype(BF)
    parts = [
        jnp.concatenate([part.astype(BF), shared], axis=1) for part in cut(r_out1, n_tensor)
    ]
    moved = [by_xor(parts[z], TENSOR, z) for z in others(TENSOR)]
    r_out1 = tree_sum([parts[0]] + moved)
    sums = r_out1[:, channels:].reshape(n_sums, width)
    r_out1 = r_out1[:, :channels]

    def whole(one, one_came, two, two_came):
        mine = jnp.where(first, one, two)
        came = jnp.where(first, one_came, two_came)
        return jnp.concatenate(
            [jnp.where(first, mine, came), jnp.where(first, came, mine)], axis=0
        )

    def sent_to(owner, value):
        return lax.ppermute(value.astype(BF), PIPE, [(1 - owner, owner)]).astype(F32)

    ffn2_came = sent_to(1, r_ffn2)
    ffn1_came = sent_to(0, r_ffn1)
    g_ffn = whole(r_ffn1, ffn1_came, r_ffn2, ffn2_came)
    gate_up_grad = jnp.stack([g_ffn[:, :hidden], g_ffn[:, hidden : 2 * hidden]], axis=1)
    down_grad = g_ffn[:, 2 * hidden :].T
    r_mix1 = jnp.concatenate([r_bc, r_out1], axis=1)
    mix_came = by_xor(jnp.where(first, r_two, r_mix1).astype(BF), PIPE, 1).astype(F32)
    g_mix = whole(r_mix1, mix_came, r_two, mix_came)
    mix_in_grad = jnp.stack([g_mix[:, :channels], g_mix[:, channels : 2 * channels]], axis=1)
    mix_out_grad = g_mix[:, 2 * channels :].T
    value_grad = lax.ppermute(r_x, (PIPE, DP), [(b, a) for a, b in value_pairs])

    taps = conv_kernel.shape[0]
    sum_kernel = sums[4 : 4 + taps]
    sum_qk = sums[4 + taps, : 2 * head_size].reshape(2, head_size)

    dh0 = order.to_true(dh0).reshape(count, quarter, width)
    recv = by_xor(jnp.where(first, out2, dh0), PIPE, 1)
    ends_out = jnp.concatenate(
        [jnp.where(first, dh0, recv), jnp.where(first, recv, out2)], axis=0
    )
    return (
        ends_out[None],
        mix_in_grad[None],
        mix_out_grad[None],
        gate_up_grad[None],
        down_grad[None],
        value_grad,
        sums[0:2],
        sums[2:4],
        sum_kernel,
        sum_qk,
    )


def solution(mesh):
    return jax.shard_map(
        compute,
        mesh=mesh,
        in_specs=(
            P(PIPE, DP, TENSOR, None),
            P(PIPE, DP, None, TENSOR),
            P(PIPE, TENSOR, DP),
            P(PIPE, DP, None, TENSOR),
            P(PIPE, TENSOR, DP),
            P((PIPE, DP), TENSOR),
            P(),
            P(),
            P(),
            P(),
            P(DP, None),
        ),
        out_specs=(
            P(PIPE, DP, TENSOR, None),
            P(PIPE, DP, None, TENSOR),
            P(PIPE, TENSOR, DP),
            P(PIPE, DP, None, TENSOR),
            P(PIPE, TENSOR, DP),
            P((PIPE, DP), TENSOR),
            P(),
            P(),
            P(),
            P(),
        ),
        check_vma=False,
    )
```
